512 devices in a mesh: grp: 32 (over z_hi, x, core), dev: 16 (over z_lo, y).
Axes of the slice: x: 4, y: 4, z: 16 (z_hi: 4, z_lo: 4; z = z_hi * 4 + z_lo), core: 2. Of those that a mesh axis runs over, the one named last changes fastest.
Arguments:
- row_ptr: int32 [32, 65], P('grp'), may hold values from 0 to 2048, as said below
- col_off: int32 [32, 2048], P('grp', 'dev'), may hold values from -32 to 32, as said below
- blocks: bfloat16 [65536, 128, 128], P(('grp', 'dev')), may hold values from -0.09375 to 0.09375
- trial: bfloat16 [262144, 256], P(('grp', 'dev')), may hold values from -6 to 6
Outputs:
- filtered: bfloat16 [393216, 256], P(('grp', 'dev'))
The draws below stay inside these ranges and needn't reach their ends.
Inputs may be any that keep to these rules, and one draw needn't show every extreme that they name: row_ptr[g, 0] = 0 and row_ptr[g, 64] = 2048; every block row holds 24 to 48 nonzero blocks, both reached; in every band the 128 nonzero blocks of some device hold the last blocks of 6 rows. For every device d of a band, the block row that holds nonzero block d * 128 lies between (d - 1) * 4 and (d + 1) * 4. `col_off`: the offsets of one block row are distinct, increasing, and include -32, 0 and 32.
All inputs are finite; a program needn't handle non-finite values.
Results may differ from the reference program's by a relative error of at most 0.0095.
Values may be sent and summed in bfloat16 or wider, within the bound.
No kernel may reach another device: no remote copies, remote signals or barrier semaphores. Data moves between devices by JAX's collectives and lax.ppermute only.
A program may use at most 64 MiB of HBM per device.

```python
import jax
import jax.numpy as jnp
import numpy as np
from jax import lax

BLK = 128
M = 256
RB_DEV = 4
AVG = 32
ROW_MIN = 24
ROW_MAX = 48
DEGREE = 2
BAND = 64
HALF = 32
NB = 2048
NNZ_DEV = 128
NNZ_BAND = 2048
SPAN = 6
N_GRP = 32
N_DEV = 16


def drawn_rows():
    head_count = 2 * RB_DEV - (SPAN - 1)
    head_sum = 2 * NNZ_DEV - ROW_MIN * (SPAN - 1)
    extra = head_sum - ROW_MIN * head_count
    planted = []
    for position in range(head_count):
        added = min(extra, ROW_MAX - ROW_MIN)
        planted.append(ROW_MIN + added)
        extra = extra - added
    planted = planted + [ROW_MIN] * (SPAN - 1)
    return np.array(planted, dtype=np.int32)


def band_pattern(key):
    devices_band = BAND // RB_DEV
    total_offsets = 2 * HALF + 1
    key_split = jax.random.fold_in(key, 1)
    key_steps = jax.random.fold_in(key, 2)
    key_scores = jax.random.fold_in(key, 3)
    split_at = jax.random.randint(key_split, (), 0, devices_band - 1).astype(jnp.int32)
    row_ids = jnp.arange(BAND, dtype=jnp.int32)
    steps_up = jax.random.randint(key_steps, (BAND,), -4, 5).astype(jnp.int32)
    cut_first = split_at * RB_DEV - 1
    cut_second = (split_at + 2) * RB_DEV - 1
    steps_up = jnp.where((row_ids == cut_first) | (row_ids == cut_second) | (row_ids == BAND - 1), 0, steps_up)
    before = jnp.concatenate([jnp.zeros((1,), jnp.int32), steps_up[:-1]])
    lengths = AVG + steps_up - before
    inside = (row_ids >= split_at * RB_DEV) & (row_ids < (split_at + 2) * RB_DEV)
    planted = jnp.asarray(drawn_rows())
    placed = jnp.take(planted, jnp.clip(row_ids - split_at * RB_DEV, 0, 2 * RB_DEV - 1))
    lengths = jnp.where(inside, placed, lengths).astype(jnp.int32)
    row_ends = jnp.cumsum(lengths).astype(jnp.int32)
    pointer = jnp.concatenate([jnp.zeros((1,), jnp.int32), row_ends])
    offset_ids = jnp.arange(total_offsets, dtype=jnp.int32)
    scores = jax.random.randint(key_scores, (BAND, total_offsets), 0, 1 << 20).astype(jnp.int32) * 256 + offset_ids[None, :]
    forced = (offset_ids == 0) | (offset_ids == HALF) | (offset_ids == 2 * HALF)
    scores = scores + jnp.where(forced, 1 << 29, 0)[None, :]
    ordering = jnp.argsort(-scores, axis=1)
    ranking = jnp.argsort(ordering, axis=1)
    chosen = ranking < lengths[:, None]
    keyed = jnp.where(chosen, offset_ids[None, :], total_offsets + offset_ids[None, :])
    ascending = (jnp.argsort(keyed, axis=1) - HALF).astype(jnp.int32)
    ordinal = jnp.arange(NNZ_BAND, dtype=jnp.int32)
    row_of = jnp.sum((row_ends[None, :] <= ordinal[:, None]).astype(jnp.int32), axis=1)
    place = ordinal - jnp.take(pointer, row_of)
    offsets = jnp.take(ascending.reshape(-1), row_of * total_offsets + place)
    return (pointer.astype(jnp.int32), offsets.astype(jnp.int32))


def pattern(key):

    def one_band(band_id):
        return band_pattern(jax.random.fold_in(key, band_id))
    return jax.vmap(one_band)(jnp.arange(N_GRP, dtype=jnp.int32))


def draw_row_ptr(key, part):
    return pattern(jax.random.fold_in(key, 11))[0]


def draw_col_off(key, part):
    return pattern(jax.random.fold_in(key, 11))[1]


def level_of(stream_key, dims, split, smallest, high):
    def one(axis_at, parts):
        draws = jax.random.uniform(jax.random.fold_in(jax.random.fold_in(stream_key, 6), axis_at), (parts,), jnp.float32, smallest / len(split), high / len(split))
        return jnp.repeat(jnp.exp(draws), dims[axis_at] // parts).reshape((-1,) + (1,) * (len(dims) - axis_at - 1))

    gain = one(*split[0])
    for cut in split[1:]:
        gain = gain * one(*cut)
    return gain


def gaussian(own_key, shape, scale, limit, shards=(), kind=jnp.bfloat16):
    gain = level_of(own_key, shape, shards, -0.22, 0.18) if shards else 1.0
    drawn = jax.random.normal(own_key, shape, jnp.float32) * scale * gain
    return jnp.minimum(jnp.maximum(drawn, -limit), limit).astype(kind)


def setup_inputs(seed: int = 0) -> dict:
    splits = jax.random.split(jax.random.key(seed), 5)
    row_ptr = draw_row_ptr(jax.random.fold_in(splits[4], 71), 0)
    col_off = draw_col_off(jax.random.fold_in(splits[4], 71), 0)
    blocks = gaussian(splits[2], (N_GRP * NNZ_BAND, BLK, BLK), (AVG * BLK) ** -0.5, 0.09375, ((0, 512),))
    trial = gaussian(splits[3], (NB * BLK, M), 1.0, 6.0, ((0, 512),))
    return {"row_ptr": row_ptr, "col_off": col_off, "blocks": blocks, "trial": trial}


filter_center = 0.5
filter_halfwidth = 1.5
piece_rows = 256


def count_ends(row_ends, limits):
    return jnp.sum((row_ends[None, :] <= limits[:, None]).astype(jnp.int32), axis=1)


def band_sums(window, pointer, offsets, matrices):
    row_ends = pointer[1:]
    ordinal = jnp.arange(NNZ_BAND, dtype=jnp.int32)
    row_of = count_ends(row_ends, ordinal)
    wanted = (row_of + offsets + HALF).astype(jnp.int32)
    turns = NNZ_BAND // piece_rows

    def one_turn(running, turn_index):
        offset_rows = (turn_index * piece_rows).astype(jnp.int32)
        columns = lax.dynamic_slice_in_dim(wanted, offset_rows, piece_rows)
        targets = lax.dynamic_slice_in_dim(row_of, offset_rows, piece_rows)
        pieces = lax.dynamic_slice_in_dim(matrices, offset_rows, piece_rows, 0).astype(jnp.float32)
        picked = jnp.take(window, columns, axis=0).astype(jnp.float32)
        products = jnp.einsum("pij,pjm->pim", pieces, picked)
        return running + jax.ops.segment_sum(products, targets, num_segments=BAND), None

    initial = jnp.zeros((BAND, BLK, M), jnp.float32)
    return lax.scan(one_turn, initial, jnp.arange(turns, dtype=jnp.int32))[0]


def reference(row_ptr, col_off, blocks, trial):
    current = trial.reshape(NB, BLK, M)
    matrices = blocks.reshape(N_GRP, NNZ_BAND, BLK, BLK)
    band_ids = jnp.arange(N_GRP, dtype=jnp.int32)

    def product(state):
        def one_band(inputs):
            band_id, pointer, offsets, pieces = inputs
            rows = (band_id * BAND - HALF + jnp.arange(BAND + 2 * HALF, dtype=jnp.int32)) % NB
            window = jnp.take(state, rows.astype(jnp.int32), axis=0)
            return band_sums(window, pointer, offsets, pieces)

        return lax.map(one_band, (band_ids, row_ptr, col_off, matrices)).reshape(NB, BLK, M)

    older = current
    for degree in range(DEGREE):
        row_sums = product(current)
        present = current.astype(jnp.float32)
        if degree == 0:
            updated = (row_sums - filter_center * present) / filter_halfwidth
        else:
            updated = 2.0 * (row_sums - filter_center * present) / filter_halfwidth - older.astype(jnp.float32)
        older = current
        current = lax.optimization_barrier(updated.astype(jnp.bfloat16))

    row_ends = row_ptr[:, 1:]
    marks = jnp.arange(N_DEV + 1, dtype=jnp.int32) * NNZ_DEV
    firsts = jnp.sum((row_ends[:, None, :] <= marks[None, :, None]).astype(jnp.int32), axis=2)
    starting = firsts[:, :-1]
    counted = firsts[:, 1:] - firsts[:, :-1]
    slot_ids = jnp.arange(SPAN, dtype=jnp.int32)
    local_rows = starting[:, :, None] + slot_ids[None, None, :]
    filled = slot_ids[None, None, :] < counted[:, :, None]
    global_rows = band_ids[:, None, None] * BAND + jnp.minimum(local_rows, BAND - 1)
    chosen = jnp.take(current, global_rows.reshape(-1).astype(jnp.int32), axis=0)
    chosen = chosen.reshape(N_GRP, N_DEV, SPAN, BLK, M)
    chosen = jnp.where(filled[:, :, :, None, None], chosen, jnp.zeros((), jnp.bfloat16))
    return chosen.reshape(N_GRP * N_DEV * SPAN * BLK, M)
```

```python
import jax
import jax.numpy as jnp
from jax import lax
from jax.experimental import pallas as pl
from jax.experimental.pallas import tpu as pltpu
from jax.sharding import PartitionSpec as P


BLK = 128
VEC = 256
SPAN = 6
HOME = 4
NNZ = 128
ROWS = 64
HALF = 32
WIN = ROWS + 2 * HALF
PLANES = 16
CENTER = 0.5
INV = 1.0 / 1.5
BF = jnp.bfloat16
F32 = jnp.float32
AXES = ("grp", "dev")


def place(plane, core, zl, y):
    return ((plane % PLANES) * 2 + core) * 16 + zl * 4 + y


def each():
    for plane in range(PLANES):
        for core in range(2):
            for zl in range(4):
                for y in range(4):
                    yield plane, core, zl, y


def joins_halo(core, zl):
    return (core == 0 and zl < 2) or (core == 1 and zl >= 2)


def shift_z(step):
    return [(place(p, c, z, y), place(p, c, (z + step) % 4, y)) for p, c, z, y in each()]


def shift_y(step, halo=False):
    return [
        (place(p, c, z, y), place(p, c, z, (y + step) % 4))
        for p, c, z, y in each()
        if not halo or joins_halo(c, z)
    ]


def swap_core():
    return [(place(p, c, z, y), place(p, 1 - c, z, y)) for p, c, z, y in each()]


def shift_dev(step):
    return [
        (g * 16 + d, g * 16 + d + step) for g in range(32) for d in range(16) if 0 <= d + step < 16
    ]


def halo_in(first):
    low = ((3, 0), (2, 1)) if first else ((2, 0), (3, 1))
    pairs = []
    for p in range(PLANES):
        for y in range(4):
            for source, target in low:
                pairs.append((place(p - 1, 1, source, y), place(p, 0, target, y)))
                pairs.append((place(p + 1, 0, 3 - source, y), place(p, 1, 3 - target, y)))
    return pairs


def edge_one():
    pairs = []
    for p in range(PLANES):
        pairs.append((place(p - 1, 1, 3, 3), place(p, 0, 2, 0)))
        pairs.append((place(p + 1, 0, 0, 0), place(p, 1, 1, 3)))
    return pairs


def edge_two():
    pairs = []
    for p in range(PLANES):
        pairs.append((place(p + 1, 0, 0, 0), place(p, 1, 1, 2)))
        pairs.append((place(p + 1, 0, 0, 1), place(p, 1, 1, 3)))
    return pairs


def send(value, pairs):
    return lax.ppermute(value, AXES, pairs)


def gather_pieces(shard, core, zl, y):
    arrays = []
    pieces = []

    def slot(group, step):
        return (8 + group * 4 + jnp.mod(y - step, 4)) * HOME

    def add(array, entries):
        for entry, rows, start in entries:
            pieces.append((len(arrays), entry, rows, start))
        arrays.append(array)

    first_pair = shard[:2]
    second_pair = shard[2:]
    halo_a = send(shard, halo_in(True))
    halo_b = send(shard, halo_in(False))
    columns = []
    for color in (first_pair, second_pair):
        columns.append(jnp.stack([color] + [send(color, shift_z(s)) for s in (1, 2, 3)]))
    halo = jnp.stack([halo_a, halo_b])
    swapped = []
    for which, column in enumerate(columns):
        up = send(column, shift_y(1))
        down = send(column, shift_y(-1))
        far = send(up, shift_y(1)) if which == 0 else send(down, shift_y(-1))
        for step, array in enumerate((column, up, far, down)):
            entries = []
            for s in range(4):
                entries.append((s, 2, slot(jnp.mod(zl - s, 4), step) + 2 * which))
            add(array, entries)
        base = jnp.where(core == 0, 2, 0)
        picks = [jnp.mod(zl - base - j, 4) for j in range(2)]
        outgoing = jnp.stack(
            [
                lax.dynamic_index_in_dim(array, pick, 0, keepdims=False)
                for array in (column, up, far, down)
                for pick in picks
            ]
        )
        swapped.append(send(outgoing, swap_core()))
    for which, array in enumerate(swapped):
        entries = []
        for step in range(4):
            for j in range(2):
                group = jnp.where(core == 0, 4 + j, j - 2)
                entries.append((step * 2 + j, 2, slot(group, step) + 2 * which))
        add(array, entries)
    member = jnp.where(core == 0, zl < 2, zl >= 2)
    outer = jnp.logical_or(zl == 0, zl == 3)
    near = jnp.where(core == 0, -1, 4)
    other = jnp.where(core == 0, -2, 5)
    group_a = jnp.where(outer, near, other)
    group_b = jnp.where(outer, other, near)
    halo_arrays = [halo] + [send(halo, shift_y(s, True)) for s in (1, 2, 3)]
    for step, array in enumerate(halo_arrays):
        entries = []
        for entry, group in enumerate((group_a, group_b)):
            entries.append((entry, 4, jnp.where(member, slot(group, step), -1)))
        add(array, entries)
    dev = zl * 4 + y
    low_edge = jnp.logical_and(core == 0, dev == 8)
    high_edge = jnp.logical_and(core == 1, dev == 7)
    high_next = jnp.logical_and(core == 1, dev == 6)
    edge_a = send(shard, edge_one())
    edge_b = send(shard[:1], edge_two())
    add(edge_a[None], [(0, 4, jnp.where(low_edge, 28, jnp.where(high_edge, 96, -1)))])
    add(edge_b[None], [(0, 1, jnp.where(high_next, 96, jnp.where(high_edge, 100, -1)))])
    return arrays, pieces


def block_products(scalars, blocks, arrays, layout, window, held, total, copy_sem, block_sem):
    loads = []
    for at, (array, entry, rows) in enumerate(layout):
        start = scalars[2 * NNZ + at]
        copy = pltpu.make_async_copy(
            arrays[array].at[entry],
            window.at[pl.ds(jnp.maximum(start, 0), rows)],
            copy_sem.at[at],
        )
        loads.append((start, copy))
        pl.when(start >= 0)(copy.start)
    whole = pltpu.make_async_copy(blocks, held, block_sem.at[0])
    whole.start()
    total[...] = jnp.zeros(total.shape, F32)
    whole.wait()
    for start, copy in loads:
        pl.when(start >= 0)(copy.wait)

    def one(p, carry):
        row = scalars[NNZ + p]
        total[row] += jnp.dot(held[p], window[scalars[p]], preferred_element_type=F32)
        return carry

    lax.fori_loop(0, NNZ, one, 0, unroll=8)


def call_products(body, scalars, blocks, pieces, arrays, extra, outs, touched):
    layout = [(array, entry, rows) for array, entry, rows, _ in pieces]
    table = jnp.concatenate(
        [scalars[0], scalars[1], jnp.stack([jnp.asarray(p[3], jnp.int32) for p in pieces]), scalars[2]]
    ).astype(jnp.int32)
    count = len(arrays)
    tail_at = 2 * NNZ + len(pieces)

    def kernel(*refs):
        table_ref, block_ref = refs[0], refs[1]
        array_refs = refs[2 : 2 + count]
        extra_refs = refs[2 + count : 2 + count + len(extra)]
        out_refs = refs[2 + count + len(extra) : 2 + count + len(extra) + len(outs)]
        window, held, total, copy_sem, block_sem = refs[2 + count + len(extra) + len(outs) :]
        block_products(
            table_ref, block_ref, array_refs, layout, window, held, total, copy_sem, block_sem
        )
        body(table_ref, tail_at, window, total, extra_refs, out_refs)

    any_spec = pl.BlockSpec(memory_space=pl.ANY)
    vmem = pl.BlockSpec(memory_space=pltpu.VMEM)
    return pl.pallas_call(
        kernel,
        out_shape=outs,
        in_specs=[pl.BlockSpec(memory_space=pltpu.SMEM)]
        + [any_spec] * (1 + count)
        + [vmem] * len(extra),
        out_specs=[vmem] * len(outs),
        scratch_shapes=[
            pltpu.VMEM((WIN, BLK, VEC), BF),
            pltpu.VMEM((NNZ, BLK, BLK), BF),
            pltpu.VMEM((touched, BLK, VEC), F32),
            pltpu.SemaphoreType.DMA((len(pieces),)),
            pltpu.SemaphoreType.DMA((1,)),
        ],
        compiler_params=pltpu.CompilerParams(vmem_limit_bytes=40 * 1024 * 1024),
    )(table, blocks, *arrays, *extra)


def body_first(table, at, window, total, extra, outs):
    low, own, high, over, older = outs
    first = table[at]
    low[...] = total[0:4].astype(BF)
    own[...] = total[4:8]
    high[...] = total[8:12].astype(BF)
    over[...] = total[12:13].astype(BF)
    for s in range(SPAN):
        older[s] = window[first + HALF + s]


def body_second(table, at, window, total, extra, outs):
    (older,) = extra
    done, tail, head = outs
    first, finished, last = table[at], table[at + 1], table[at + 2]
    for s in range(SPAN):
        present = window[first + HALF + s].astype(F32)
        value = 2.0 * (total[s] - CENTER * present) * INV - older[s].astype(F32)
        value = jnp.where(s < finished, value, 0.0)
        done[s] = value.astype(BF)
        if s == 0:
            head[...] = value
    tail[...] = jnp.where(last == finished, total[last], 0.0).astype(BF)


def local(row_ptr, col_off, blocks, trial):
    row_ends = row_ptr[0, 1:]
    group = lax.axis_index("grp")
    member = lax.axis_index("dev")
    core = group % 2
    zl = member // 4
    y = member % 4
    first_nnz = member * NNZ
    ordinal = first_nnz + jnp.arange(NNZ, dtype=jnp.int32)
    row_of = jnp.sum((row_ends[None, :] <= ordinal[:, None]).astype(jnp.int32), axis=1)
    first_row = row_of[0]
    finished = jnp.sum(
        jnp.logical_and(row_ends > first_nnz, row_ends <= first_nnz + NNZ).astype(jnp.int32)
    )
    last_local = row_of[NNZ - 1] - first_row
    wanted = row_of + col_off[0] + HALF
    ends = jnp.stack([first_row, finished, last_local])
    shard = trial.reshape(HOME, BLK, VEC)

    shape = jax.ShapeDtypeStruct
    arrays, pieces = gather_pieces(shard, core, zl, y)
    low, own, high, over, older = call_products(
        body_first,
        (wanted, row_of - (HOME * member - HOME), ends),
        blocks,
        pieces,
        arrays,
        [],
        [
            shape((4, BLK, VEC), BF),
            shape((4, BLK, VEC), F32),
            shape((4, BLK, VEC), BF),
            shape((1, BLK, VEC), BF),
            shape((SPAN, BLK, VEC), BF),
        ],
        13,
    )
    sums = own + send(low, shift_dev(-1)).astype(F32) + send(high, shift_dev(1)).astype(F32)
    sums = sums.at[:1].add(send(over, shift_dev(2)).astype(F32))
    updated = ((sums - CENTER * shard.astype(F32)) / 1.5).astype(BF)

    arrays, pieces = gather_pieces(updated, core, zl, y)
    done, tail, head = call_products(
        body_second,
        (wanted, row_of - first_row, ends),
        blocks,
        pieces,
        arrays,
        [older],
        [shape((SPAN, BLK, VEC), BF), shape((BLK, VEC), BF), shape((BLK, VEC), F32)],
        7,
    )
    carried = send(tail, shift_dev(1)).astype(F32)
    top = head + jnp.where(finished > 0, 2.0 * carried * INV, 0.0)
    done = done.at[0].set(top.astype(BF))
    return done.reshape(SPAN * BLK, VEC)


def solution(mesh):
    in_specs = (
        P("grp", None),
        P("grp", "dev"),
        P(("grp", "dev"), None, None),
        P(("grp", "dev"), None),
    )
    out_specs = P(("grp", "dev"), None)
    return jax.shard_map(local, mesh=mesh, in_specs=in_specs, out_specs=out_specs, check_vma=False)
```

```python
import jax
import jax.numpy as jnp
from jax import lax
from jax.experimental import pallas as pl
from jax.experimental.pallas import tpu as pltpu
from jax.sharding import PartitionSpec as P


BLK = 128
VEC = 256
SPAN = 6
HOME = 4
NNZ = 128
ROWS = 64
HALF = 32
DEPTH = 4
WIN = ROWS + 2 * HALF
DEVICES = 512
CENTER = 0.5
INV = 1.0 / 1.5
BF = jnp.bfloat16
F32 = jnp.float32
AXES = ("grp", "dev")


def shift_all(step):
    return [(g, (g + step) % DEVICES) for g in range(DEVICES)]


def shift_y(step):
    return [(g, g // 4 * 4 + (g + step) % 4) for g in range(DEVICES)]


def shift_dev(step):
    return [(g, g + step) for g in range(DEVICES) if 0 <= g % 16 + step < 16]


def edge_rows():
    down = [(g, (g + 9) % DEVICES) for g in range(DEVICES) if g % 4 == 3]
    up = [(g, (g - 9) % DEVICES) for g in range(DEVICES) if g % 4 == 0]
    return down + up


def edge_row():
    return [(g, (g - 10) % DEVICES) for g in range(DEVICES) if g % 4 < 2]


def send(value, pairs):
    return lax.ppermute(value, AXES, pairs)


def gather_pieces(shard, member):
    zl = member // 4
    y = member % 4
    arrays = []
    pieces = []

    def add(array, entries):
        for entry, rows, start in entries:
            pieces.append((len(arrays), entry, rows, start))
        arrays.append(array)

    def add_groups(array, offsets, step):
        entries = []
        for entry, offset in enumerate(offsets):
            entries.append((entry, HOME, (8 + (zl + offset) * 4 + jnp.mod(y - step, 4)) * HOME))
        add(array, entries)

    below = send(shard, shift_all(4))
    above = send(shard, shift_all(-4))
    up = send(shard, shift_y(1))
    down = send(shard, shift_y(-1))
    far_below = send(shard, shift_all(8))
    far_above = send(shard, shift_all(-8))
    across = send(shard, shift_y(2))
    for step, array in enumerate((shard, up, across, down)):
        add_groups(array[None], (0,), step)
    near = jnp.stack([below, above])
    far = jnp.stack([far_below, far_above])
    near_up = send(near, shift_y(1))
    near_down = send(near, shift_y(-1))
    near_across = send(near_up, shift_y(1))
    far_up = send(far, shift_y(1))
    far_down = send(far, shift_y(-1))
    far_across = send(far_down, shift_y(-1))
    for step, array in enumerate((near, near_up, near_across, near_down)):
        add_groups(array, (-1, 1), step)
    for step, array in enumerate((far, far_up, far_across, far_down)):
        add_groups(array, (-2, 2), step)
    edge_a = send(shard, edge_rows())
    edge_b = send(shard[:1], edge_row())
    slot_a = jnp.where(y == 0, member - 9, member + 9) + 8
    used_a = jnp.logical_and(jnp.logical_or(y == 0, y == 3), jnp.logical_and(slot_a >= 0, slot_a < 32))
    slot_b = member + 10 + 8
    used_b = jnp.logical_and(y >= 2, slot_b < 32)
    add(edge_a[None], [(0, HOME, jnp.where(used_a, slot_a * HOME, -1))])
    add(edge_b[None], [(0, 1, jnp.where(used_b, slot_b * HOME, -1))])
    return arrays, pieces


def block_products(table, at, shift, blocks, arrays, layout, window, held, total, copy_sem, block_sem):
    whole = pltpu.make_async_copy(blocks, held.at[pl.ds(0, NNZ)], block_sem.at[0])
    whole.start()
    loads = []
    for which, (array, entry, rows) in enumerate(layout):
        start = table[NNZ + which]
        copy = pltpu.make_async_copy(
            arrays[array].at[entry],
            window.at[pl.ds(jnp.maximum(start, 0), rows)],
            copy_sem.at[which],
        )
        loads.append((start, copy))
        pl.when(start >= 0)(copy.start)
    held[NNZ] = jnp.zeros((BLK, BLK), BF)
    total[...] = jnp.zeros(total.shape, F32)
    whole.wait()
    for start, copy in loads:
        pl.when(start >= 0)(copy.wait)

    def one_row(r, carry):
        low = table[at + 3 + r]
        high = table[at + 4 + r]

        def one_group(q, value):
            base = low + q * DEPTH
            lefts = []
            rights = []
            for i in range(DEPTH):
                p = base + i
                lefts.append(held[jnp.where(p < high, p, NNZ)])
                rights.append(window[table[jnp.minimum(p, high - 1)]])
            left = jnp.concatenate(lefts, axis=1)
            right = jnp.concatenate(rights, axis=0)
            return value + jnp.dot(left, right, preferred_element_type=F32)

        total[shift + r] = lax.fori_loop(
            0, (high - low + DEPTH - 1) // DEPTH, one_group, jnp.zeros((BLK, VEC), F32)
        )
        return carry

    lax.fori_loop(0, SPAN + 1, one_row, 0)


def call_products(body, homed, scalars, blocks, pieces, arrays, extra, outs, touched):
    layout = [(array, entry, rows) for array, entry, rows, _ in pieces]
    wanted, ends = scalars
    starts = jnp.stack([jnp.asarray(p[3], jnp.int32) for p in pieces])
    table = jnp.concatenate([wanted, starts, ends]).astype(jnp.int32)
    count = len(arrays)
    at = NNZ + len(pieces)

    def kernel(*refs):
        table_ref, block_ref = refs[0], refs[1]
        array_refs = refs[2 : 2 + count]
        extra_refs = refs[2 + count : 2 + count + len(extra)]
        out_refs = refs[2 + count + len(extra) : 2 + count + len(extra) + len(outs)]
        window, held, total, copy_sem, block_sem = refs[2 + count + len(extra) + len(outs) :]
        shift = table_ref[at + 11] if homed else 0
        block_products(
            table_ref, at, shift, block_ref, array_refs, layout, window, held, total, copy_sem, block_sem
        )
        body(table_ref, at, window, total, extra_refs, out_refs)

    hbm = pl.BlockSpec(memory_space=pltpu.HBM)
    vmem = pl.BlockSpec(memory_space=pltpu.VMEM)
    return pl.pallas_call(
        kernel,
        out_shape=outs,
        in_specs=[pl.BlockSpec(memory_space=pltpu.SMEM)] + [hbm] * (1 + count) + [vmem] * len(extra),
        out_specs=[vmem] * len(outs),
        scratch_shapes=[
            pltpu.VMEM((WIN, BLK, VEC), BF),
            pltpu.VMEM((NNZ + 1, BLK, BLK), BF),
            pltpu.VMEM((touched, BLK, VEC), F32),
            pltpu.SemaphoreType.DMA((len(pieces),)),
            pltpu.SemaphoreType.DMA((1,)),
        ],
        compiler_params=pltpu.CompilerParams(vmem_limit_bytes=40 * 1024 * 1024),
    )(table, blocks, *arrays, *extra)


def body_first(table, at, window, total, extra, outs):
    low, own, high, over, older = outs
    first = table[at]
    low[...] = total[0:4].astype(BF)
    own[...] = total[4:8]
    high[...] = total[8:12].astype(BF)
    over[...] = total[12:13].astype(BF)
    for s in range(SPAN):
        older[s] = window[first + HALF + s]


def body_second(table, at, window, total, extra, outs):
    (older,) = extra
    done, tail, head = outs
    first, finished, last = table[at], table[at + 1], table[at + 2]
    for s in range(SPAN):
        present = window[first + HALF + s].astype(F32)
        value = 2.0 * (total[s] - CENTER * present) * INV - older[s].astype(F32)
        value = jnp.where(s < finished, value, 0.0)
        done[s] = value.astype(BF)
        if s == 0:
            head[...] = value
    tail[...] = jnp.where(last == finished, total[last], 0.0).astype(BF)


def local(row_ptr, col_off, blocks, trial):
    row_ends = row_ptr[0, 1:]
    member = lax.axis_index("dev")
    first_nnz = member * NNZ
    ordinal = first_nnz + jnp.arange(NNZ, dtype=jnp.int32)
    row_of = jnp.sum((row_ends[None, :] <= ordinal[:, None]).astype(jnp.int32), axis=1)
    first_row = row_of[0]
    finished = jnp.sum(
        jnp.logical_and(row_ends > first_nnz, row_ends <= first_nnz + NNZ).astype(jnp.int32)
    )
    last_local = row_of[NNZ - 1] - first_row
    wanted = row_of + col_off[0] + HALF
    edges = jnp.take(row_ptr[0], jnp.minimum(first_row + jnp.arange(SPAN + 2), ROWS)) - first_nnz
    home_shift = first_row - (HOME * member - HOME)
    ends = jnp.concatenate(
        [
            jnp.stack([first_row, finished, last_local]),
            jnp.clip(edges, 0, NNZ),
            home_shift[None],
        ]
    )
    shard = trial.reshape(HOME, BLK, VEC)

    shape = jax.ShapeDtypeStruct
    arrays, pieces = gather_pieces(shard, member)
    low, own, high, over, older = call_products(
        body_first,
        True,
        (wanted, ends),
        blocks,
        pieces,
        arrays,
        [],
        [
            shape((4, BLK, VEC), BF),
            shape((4, BLK, VEC), F32),
            shape((4, BLK, VEC), BF),
            shape((1, BLK, VEC), BF),
            shape((SPAN, BLK, VEC), BF),
        ],
        15,
    )
    sums = own + send(low, shift_dev(-1)).astype(F32) + send(high, shift_dev(1)).astype(F32)
    sums = sums.at[:1].add(send(over, shift_dev(2)).astype(F32))
    updated = ((sums - CENTER * shard.astype(F32)) / 1.5).astype(BF)

    arrays, pieces = gather_pieces(updated, member)
    done, tail, head = call_products(
        body_second,
        False,
        (wanted, ends),
        blocks,
        pieces,
        arrays,
        [older],
        [shape((SPAN, BLK, VEC), BF), shape((BLK, VEC), BF), shape((BLK, VEC), F32)],
        7,
    )
    carried = send(tail, shift_dev(1)).astype(F32)
    top = head + jnp.where(finished > 0, 2.0 * carried * INV, 0.0)
    done = done.at[0].set(top.astype(BF))
    return done.reshape(SPAN * BLK, VEC)


def solution(mesh):
    in_specs = (
        P("grp", None),
        P("grp", "dev"),
        P(("grp", "dev"), None, None),
        P(("grp", "dev"), None),
    )
    out_specs = P(("grp", "dev"), None)
    return jax.shard_map(local, mesh=mesh, in_specs=in_specs, out_specs=out_specs, check_vma=False)
```

```python
import jax
import jax.numpy as jnp
from jax import lax
from jax.experimental import pallas as pl
from jax.experimental.pallas import tpu as pltpu
from jax.sharding import PartitionSpec as P


BLK = 128
VEC = 256
SPAN = 6
HOME = 4
NNZ = 128
ROWS = 64
DEPTH = 4
HALF = 32
WIN = ROWS + 2 * HALF
DEVICES = 512
CENTER = 0.5
INV = 1.0 / 1.5
BF = jnp.bfloat16
F32 = jnp.float32
AXES = ("grp", "dev")


def swap_z(odd):
    pairs = []
    for g in range(DEVICES):
        group = g // 4
        other = group + 1 if group % 2 == odd else group - 1
        pairs.append((g, (other * 4 + g % 4) % DEVICES))
    return pairs


def swap_y(odd):
    return [(g, g // 4 * 4 + (3 - g % 4 if odd else (g % 4) ^ 1)) for g in range(DEVICES)]


def shift_dev(step):
    return [(g, g + step) for g in range(DEVICES) if 0 <= g % 16 + step < 16]


def swap_dev(odd):
    pairs = []
    for g in range(DEVICES):
        other = g + 1 if g % 2 == odd else g - 1
        if other // 16 == g // 16:
            pairs.append((g, other))
    return pairs


def edge_rows():
    down = [(g, (g + 9) % DEVICES) for g in range(DEVICES) if g % 4 == 3]
    up = [(g, (g - 9) % DEVICES) for g in range(DEVICES) if g % 4 == 0]
    return down + up + [(g, (g - 11) % DEVICES) for g in range(DEVICES) if g % 4 == 1]


def send(value, pairs):
    return lax.ppermute(value, AXES, pairs)


def gather_arrays(shard, member, held_back):
    side = 1 - 2 * (member // 4 % 2)
    lower = member % 4 < 2
    next_a = send(shard, swap_z(0))
    next_b = send(shard, swap_z(1))
    edge = send(shard, edge_rows())
    first = jnp.stack([shard, next_a])
    far_b = send(next_a, swap_z(1))
    far_a = send(next_b, swap_z(0))
    first_a = send(first, swap_y(0))
    first_b = send(first, swap_y(1))
    first_x = send(first_a, swap_y(1))
    second_a = send(next_b, swap_y(0))
    second_b = send(next_b, swap_y(1))
    second_x = send(second_b, swap_y(0))
    third = jnp.stack([far_a, far_b])
    third_a = send(third, swap_y(0))
    third_b = send(third, swap_y(1))
    wants_far_b = lower == (side == 1)
    wanted = jnp.where(wants_far_b, third_b[1], third_b[0])
    other = jnp.where(wants_far_b, third_b[0, :1], third_b[1, :1])
    last = send(jnp.concatenate([wanted, jnp.where(lower, other, edge[:1])]), swap_y(0))
    arrays = [first, first_a, first_b, first_x]
    arrays += [next_b, second_a, second_b, second_x, third, third_a, third_b, last, edge]
    arrays = [array.reshape(-1, BLK, VEC) for array in arrays]
    if held_back is None:
        return arrays, None
    return arrays, lax.optimization_barrier((held_back, first))[0]


def window_pieces(member):
    zl = member >> 2
    y = member & 3
    side = 1 - 2 * (zl & 1)

    def at(offset, source):
        return (8 + (zl + offset) * 4 + source) * HOME

    pieces = []
    for array, source in enumerate((y, y ^ 1, 3 - y, y ^ 2)):
        pieces += [(array, 4 * i, HOME, at(offset, source)) for i, offset in enumerate((0, side))]
        pieces.append((4 + array, 0, HOME, at(-side, source)))
    for array, source in enumerate((y, y ^ 1, 3 - y)):
        offsets = (2 * side, -2 * side)
        pieces += [(8 + array, 4 * i, HOME, at(offset, source)) for i, offset in enumerate(offsets)]
    lower = y < 2
    pieces.append((11, 0, HOME, at(jnp.where(lower, -2, 2), y ^ 2)))
    single = jnp.where(lower, at(2, y ^ 2), at(3, y - 2))
    pieces.append((11, HOME, 1, jnp.where(single < WIN, single, -1)))
    whole = jnp.where(y == 0, at(-3, 3), jnp.where(y == 3, at(3, 0), -1))
    pieces.append((12, 0, HOME, jnp.where(whole < WIN, whole, -1)))
    return pieces


def fetch(blocks):
    def kernel(source, target, sem):
        copy = pltpu.make_async_copy(source, target, sem.at[0])
        copy.start()
        copy.wait()

    return pl.pallas_call(
        kernel,
        out_shape=pltpu.VMEM(blocks.shape, blocks.dtype),
        in_specs=[pl.BlockSpec(memory_space=pltpu.HBM)],
        out_specs=pl.BlockSpec(memory_space=pltpu.VMEM),
        scratch_shapes=[pltpu.SemaphoreType.DMA((1,))],
        compiler_params=pltpu.CompilerParams(vmem_limit_bytes=1024 * 1024),
    )(blocks)


def block_products(pointer, offsets, member, homed, held, arrays, window, total, copy_sem):
    loads = []
    for which, (array, entry, rows, start) in enumerate(window_pieces(member)):
        copy = pltpu.make_async_copy(
            arrays[array].at[pl.ds(entry, rows)],
            window.at[pl.ds(jnp.maximum(start, 0), rows)],
            copy_sem.at[which],
        )
        loads.append((start, copy))
        pl.when(start >= 0)(copy.start)
    total[...] = jnp.zeros(total.shape, F32)
    first_nnz = member * NNZ
    first_row = jnp.int32(0)
    for r in range(ROWS):
        first_row += (pointer[0, r + 1] <= first_nnz).astype(jnp.int32)
    shift = first_row - (HOME * member - HOME) if homed else 0
    finished = jnp.int32(0)
    for r in range(SPAN + 1):
        end = pointer[0, jnp.minimum(first_row + r + 1, ROWS)]
        ends_here = jnp.logical_and(first_row + r < ROWS, end <= first_nnz + NNZ)
        finished += ends_here.astype(jnp.int32)
    for start, copy in loads:
        pl.when(start >= 0)(copy.wait)

    def one_row(r, carry):
        row = first_row + r
        low = jnp.clip(pointer[0, jnp.minimum(row, ROWS)] - first_nnz, 0, NNZ)
        high = jnp.clip(pointer[0, jnp.minimum(row + 1, ROWS)] - first_nnz, 0, NNZ)

        def one_group(q, value):
            base = low + q * DEPTH
            lefts = []
            rights = []
            for i in range(DEPTH):
                p = base + i
                inside = jnp.minimum(p, high - 1)
                block = held[inside]
                lefts.append(block if i == 0 else jnp.where(p < high, block, jnp.zeros_like(block)))
                rights.append(window[row + offsets[0, inside] + HALF])
            left = jnp.concatenate(lefts, axis=1)
            right = jnp.concatenate(rights, axis=0)
            return value + jnp.dot(left, right, preferred_element_type=F32)

        total[shift + r] = lax.fori_loop(
            0, (high - low + DEPTH - 1) // DEPTH, one_group, jnp.zeros((BLK, VEC), F32)
        )
        return carry

    lax.fori_loop(0, SPAN + 1, one_row, 0)
    return first_row, finished


def call_products(body, homed, scalars, held, arrays, extra, outs, touched):
    count = len(arrays)

    def kernel(*refs):
        pointer, offsets, place, held_ref = refs[:4]
        array_refs = refs[4 : 4 + count]
        extra_refs = refs[4 + count : 4 + count + len(extra)]
        out_refs = refs[4 + count + len(extra) : 4 + count + len(extra) + len(outs)]
        window, total, copy_sem = refs[4 + count + len(extra) + len(outs) :]
        member = place[0]
        first_row, finished = block_products(
            pointer, offsets, member, homed, held_ref, array_refs, window, total, copy_sem
        )
        body(member, first_row, finished, window, total, extra_refs, out_refs)

    hbm = pl.BlockSpec(memory_space=pltpu.HBM)
    vmem = pl.BlockSpec(memory_space=pltpu.VMEM)
    smem = pl.BlockSpec(memory_space=pltpu.SMEM)
    return pl.pallas_call(
        kernel,
        out_shape=outs,
        in_specs=[smem] * 3 + [vmem] + [hbm] * count + [vmem] * len(extra),
        out_specs=[vmem] * len(outs),
        scratch_shapes=[
            pltpu.VMEM((WIN, BLK, VEC), BF),
            pltpu.VMEM((touched, BLK, VEC), F32),
            pltpu.SemaphoreType.DMA((len(window_pieces(0)),)),
        ],
        compiler_params=pltpu.CompilerParams(vmem_limit_bytes=40 * 1024 * 1024),
    )(*scalars, held, *arrays, *extra)


def body_first(member, first, finished, window, total, extra, outs):
    to_pair, own, to_next, over, older = outs
    even = (member & 1) == 0
    to_pair[...] = total[pl.ds(jnp.where(even, 8, 0), HOME)].astype(BF)
    own[...] = total[4:8]
    to_next[...] = total[pl.ds(jnp.where(even, 0, 8), HOME)].astype(BF)
    over[...] = total[12:13].astype(BF)
    for s in range(SPAN):
        older[s] = window[first + HALF + s]


def body_second(member, first, finished, window, total, extra, outs):
    (older,) = extra
    done, tail, head = outs
    for s in range(SPAN):
        present = window[first + HALF + s].astype(F32)
        value = 2.0 * (total[s] - CENTER * present) * INV - older[s].astype(F32)
        value = jnp.where(s < finished, value, 0.0)
        done[s] = value.astype(BF)
        if s == 0:
            head[...] = value
    tail[...] = total[jnp.minimum(finished, SPAN)].astype(BF)


def local(row_ptr, col_off, blocks, trial):
    member = lax.axis_index("dev")
    scalars = (row_ptr, col_off, member[None].astype(jnp.int32))
    shard = trial.reshape(HOME, BLK, VEC)

    shape = jax.ShapeDtypeStruct
    arrays, blocks = gather_arrays(shard, member, blocks)
    held = fetch(blocks)
    to_pair, own, to_next, over, older = call_products(
        body_first,
        True,
        scalars,
        held,
        arrays,
        [],
        [
            shape((4, BLK, VEC), BF),
            shape((4, BLK, VEC), F32),
            shape((4, BLK, VEC), BF),
            shape((1, BLK, VEC), BF),
            shape((SPAN, BLK, VEC), BF),
        ],
        15,
    )
    over = send(over, shift_dev(2))
    by_pair = send(to_pair, swap_dev(0))
    by_next = send(to_next, swap_dev(1))
    sums = own + by_pair.astype(F32) + by_next.astype(F32)
    sums = sums.at[:1].add(over.astype(F32))
    updated = ((sums - CENTER * shard.astype(F32)) / 1.5).astype(BF)

    arrays, _ = gather_arrays(updated, member, None)
    done, tail, head = call_products(
        body_second,
        False,
        scalars,
        held,
        arrays,
        [older],
        [shape((SPAN, BLK, VEC), BF), shape((BLK, VEC), BF), shape((BLK, VEC), F32)],
        7,
    )
    carried = send(tail, shift_dev(1)).astype(F32)
    top = head + 2.0 * carried * INV
    done = done.at[0].set(top.astype(BF))
    return done.reshape(SPAN * BLK, VEC)


def solution(mesh):
    in_specs = (
        P("grp", None),
        P("grp", "dev"),
        P(("grp", "dev"), None, None),
        P(("grp", "dev"), None),
    )
    out_specs = P(("grp", "dev"), None)
    return jax.shard_map(local, mesh=mesh, in_specs=in_specs, out_specs=out_specs, check_vma=False)
```

```python
import jax
import jax.numpy as jnp
from jax import lax
from jax.experimental import pallas as pl
from jax.experimental.pallas import tpu as pltpu
from jax.sharding import PartitionSpec as P


BLK = 128
VEC = 256
SPAN = 6
HOME = 4
NNZ = 128
ROWS = 64
DEPTH = 16
HALF = 32
WIN = ROWS + 2 * HALF
DEVICES = 512
CENTER = 0.5
INV = 1.0 / 1.5
BF = jnp.bfloat16
F32 = jnp.float32
AXES = ("grp", "dev")


def swap_z(odd):
    pairs = []
    for g in range(DEVICES):
        group = g // 4
        other = group + 1 if group % 2 == odd else group - 1
        pairs.append((g, (other * 4 + g % 4) % DEVICES))
    return pairs


def swap_y(odd):
    return [(g, g // 4 * 4 + (3 - g % 4 if odd else (g % 4) ^ 1)) for g in range(DEVICES)]


def shift_dev(step):
    return [(g, g + step) for g in range(DEVICES) if 0 <= g % 16 + step < 16]


def cross_y():
    return [(g, g ^ 2) for g in range(DEVICES)]


def swap_dev(odd):
    pairs = []
    for g in range(DEVICES):
        other = g + 1 if g % 2 == odd else g - 1
        if other // 16 == g // 16:
            pairs.append((g, other))
    return pairs


def edge_rows():
    down = [(g, (g + 9) % DEVICES) for g in range(DEVICES) if g % 4 == 3]
    up = [(g, (g - 9) % DEVICES) for g in range(DEVICES) if g % 4 == 0]
    return down + up + [(g, (g - 11) % DEVICES) for g in range(DEVICES) if g % 4 == 1]


def send(value, pairs):
    return lax.ppermute(value, AXES, pairs)


def gather_arrays(shard, member, held_back):
    side = 1 - 2 * (member // 4 % 2)
    lower = member % 4 < 2
    next_a = send(shard, swap_z(0))
    next_b = send(shard, swap_z(1))
    edge = send(shard, edge_rows())
    first = jnp.stack([shard, next_a])
    far_b = send(next_a, swap_z(1))
    far_a = send(next_b, swap_z(0))
    first_a = send(first, swap_y(0))
    first_b = send(first, swap_y(1))
    first_x = send(first, cross_y())
    second_a = send(next_b, swap_y(0))
    second_b = send(next_b, swap_y(1))
    second_x = send(jnp.concatenate([second_b, edge[:1]]), swap_y(0))
    third = jnp.stack([far_a, far_b])
    third_a = send(third, swap_y(0))
    third_b = send(third, swap_y(1))
    sends_far_b = lower == (side == 1)
    wanted = jnp.where(sends_far_b, far_a, far_b)
    other = jnp.where(sends_far_b, far_b, far_a)
    last = send(jnp.concatenate([wanted, other[:1]]), cross_y())
    arrays = [first, first_a, first_b, first_x]
    arrays += [next_b, second_a, second_b, second_x, third, third_a, third_b, last, edge]
    arrays = [array.reshape(-1, BLK, VEC) for array in arrays]
    if held_back is None:
        return arrays, None
    return arrays, lax.optimization_barrier((held_back, first))[0]


def window_pieces(member):
    zl = member >> 2
    y = member & 3
    side = 1 - 2 * (zl & 1)

    def at(offset, source):
        return (8 + (zl + offset) * 4 + source) * HOME

    pieces = []
    for array, source in enumerate((y, y ^ 1, 3 - y, y ^ 2)):
        pieces += [(array, 4 * i, HOME, at(offset, source)) for i, offset in enumerate((0, side))]
        pieces.append((4 + array, 0, HOME, at(-side, source)))
    for array, source in enumerate((y, y ^ 1, 3 - y)):
        offsets = (2 * side, -2 * side)
        pieces += [(8 + array, 4 * i, HOME, at(offset, source)) for i, offset in enumerate(offsets)]
    lower = y < 2
    pieces.append((11, 0, HOME, at(jnp.where(lower, -2, 2), y ^ 2)))
    pieces.append((11, HOME, 1, jnp.where(lower, at(2, y ^ 2), -1)))
    next_up = at(3, y - 2)
    reaches = jnp.logical_and(y >= 2, next_up < WIN)
    pieces.append((7, HOME, 1, jnp.where(reaches, next_up, -1)))
    whole = jnp.where(y == 0, at(-3, 3), jnp.where(y == 3, at(3, 0), -1))
    pieces.append((12, 0, HOME, jnp.where(whole < WIN, whole, -1)))
    return pieces


def fetch(blocks):
    def kernel(source, target, sem):
        copy = pltpu.make_async_copy(source, target, sem.at[0])
        copy.start()
        copy.wait()

    return pl.pallas_call(
        kernel,
        out_shape=pltpu.VMEM(blocks.shape, blocks.dtype),
        in_specs=[pl.BlockSpec(memory_space=pltpu.HBM)],
        out_specs=pl.BlockSpec(memory_space=pltpu.VMEM),
        scratch_shapes=[pltpu.SemaphoreType.DMA((1,))],
        compiler_params=pltpu.CompilerParams(vmem_limit_bytes=1024 * 1024),
    )(blocks)


def block_products(pointer, offsets, member, homed, held, arrays, window, total, copy_sem):
    loads = []
    for which, (array, entry, rows, start) in enumerate(window_pieces(member)):
        copy = pltpu.make_async_copy(
            arrays[array].at[pl.ds(entry, rows)],
            window.at[pl.ds(jnp.maximum(start, 0), rows)],
            copy_sem.at[which],
        )
        loads.append((start, copy))
        pl.when(start >= 0)(copy.start)
    total[...] = jnp.zeros(total.shape, F32)
    first_nnz = member * NNZ
    first_row = jnp.int32(0)
    for r in range(ROWS):
        first_row += (pointer[0, r + 1] <= first_nnz).astype(jnp.int32)
    shift = first_row - (HOME * member - HOME) if homed else 0
    finished = jnp.int32(0)
    for r in range(SPAN + 1):
        end = pointer[0, jnp.minimum(first_row + r + 1, ROWS)]
        ends_here = jnp.logical_and(first_row + r < ROWS, end <= first_nnz + NNZ)
        finished += ends_here.astype(jnp.int32)
    for start, copy in loads:
        pl.when(start >= 0)(copy.wait)

    def one_row(r, carry):
        row = first_row + r
        low = jnp.clip(pointer[0, jnp.minimum(row, ROWS)] - first_nnz, 0, NNZ)
        high = jnp.clip(pointer[0, jnp.minimum(row + 1, ROWS)] - first_nnz, 0, NNZ)

        def one_group(q, value):
            base = low + q * DEPTH
            lefts = []
            rights = []
            for i in range(DEPTH):
                p = base + i
                inside = jnp.minimum(p, high - 1)
                block = held[inside]
                lefts.append(block if i == 0 else jnp.where(p < high, block, jnp.zeros_like(block)))
                rights.append(window[row + offsets[0, inside] + HALF])
            left = jnp.concatenate(lefts, axis=1)
            right = jnp.concatenate(rights, axis=0)
            return value + jnp.dot(left, right, preferred_element_type=F32)

        total[shift + r] = lax.fori_loop(
            0, (high - low + DEPTH - 1) // DEPTH, one_group, jnp.zeros((BLK, VEC), F32)
        )
        return carry

    lax.fori_loop(0, SPAN + 1, one_row, 0)
    return first_row, finished


def call_products(body, homed, scalars, held, arrays, extra, outs, touched):
    count = len(arrays)

    def kernel(*refs):
        pointer, offsets, place, held_ref = refs[:4]
        array_refs = refs[4 : 4 + count]
        extra_refs = refs[4 + count : 4 + count + len(extra)]
        out_refs = refs[4 + count + len(extra) : 4 + count + len(extra) + len(outs)]
        window, total, copy_sem = refs[4 + count + len(extra) + len(outs) :]
        member = place[0]
        first_row, finished = block_products(
            pointer, offsets, member, homed, held_ref, array_refs, window, total, copy_sem
        )
        body(member, first_row, finished, window, total, extra_refs, out_refs)

    hbm = pl.BlockSpec(memory_space=pltpu.HBM)
    vmem = pl.BlockSpec(memory_space=pltpu.VMEM)
    smem = pl.BlockSpec(memory_space=pltpu.SMEM)
    return pl.pallas_call(
        kernel,
        out_shape=outs,
        in_specs=[smem] * 3 + [vmem] + [hbm] * count + [vmem] * len(extra),
        out_specs=[vmem] * len(outs),
        scratch_shapes=[
            pltpu.VMEM((WIN, BLK, VEC), BF),
            pltpu.VMEM((touched, BLK, VEC), F32),
            pltpu.SemaphoreType.DMA((len(window_pieces(0)),)),
        ],
        compiler_params=pltpu.CompilerParams(vmem_limit_bytes=40 * 1024 * 1024),
    )(*scalars, held, *arrays, *extra)


def body_first(member, first, finished, window, total, extra, outs):
    to_pair, own, to_next, over, older = outs
    even = (member & 1) == 0
    to_pair[...] = total[pl.ds(jnp.where(even, 8, 0), HOME)].astype(BF)
    own[...] = total[4:8]
    to_next[...] = total[pl.ds(jnp.where(even, 0, 8), HOME)].astype(BF)
    over[...] = total[12:13].astype(BF)
    for s in range(SPAN):
        older[s] = window[first + HALF + s]


def body_second(member, first, finished, window, total, extra, outs):
    (older,) = extra
    done, tail, head = outs
    for s in range(SPAN):
        present = window[first + HALF + s].astype(F32)
        value = 2.0 * (total[s] - CENTER * present) * INV - older[s].astype(F32)
        value = jnp.where(s < finished, value, 0.0)
        done[s] = value.astype(BF)
        if s == 0:
            head[...] = value
    tail[...] = total[jnp.minimum(finished, SPAN)].astype(BF)


def local(row_ptr, col_off, blocks, trial):
    member = lax.axis_index("dev")
    scalars = (row_ptr, col_off, member[None].astype(jnp.int32))
    shard = trial.reshape(HOME, BLK, VEC)

    shape = jax.ShapeDtypeStruct
    arrays, blocks = gather_arrays(shard, member, blocks)
    held = fetch(blocks)
    to_pair, own, to_next, over, older = call_products(
        body_first,
        True,
        scalars,
        held,
        arrays,
        [],
        [
            shape((4, BLK, VEC), BF),
            shape((4, BLK, VEC), F32),
            shape((4, BLK, VEC), BF),
            shape((1, BLK, VEC), BF),
            shape((SPAN, BLK, VEC), BF),
        ],
        15,
    )
    over = send(over, shift_dev(2))
    by_pair = send(to_pair, swap_dev(0))
    by_next = send(to_next, swap_dev(1))
    sums = own + by_pair.astype(F32) + by_next.astype(F32)
    sums = sums.at[:1].add(over.astype(F32))
    updated = ((sums - CENTER * shard.astype(F32)) / 1.5).astype(BF)

    arrays, _ = gather_arrays(updated, member, None)
    done, tail, head = call_products(
        body_second,
        False,
        scalars,
        held,
        arrays,
        [older],
        [shape((SPAN, BLK, VEC), BF), shape((BLK, VEC), BF), shape((BLK, VEC), F32)],
        7,
    )
    carried = send(tail, shift_dev(1)).astype(F32)
    top = head + 2.0 * carried * INV
    done = done.at[0].set(top.astype(BF))
    return done.reshape(SPAN * BLK, VEC)


def solution(mesh):
    in_specs = (
        P("grp", None),
        P("grp", "dev"),
        P(("grp", "dev"), None, None),
        P(("grp", "dev"), None),
    )
    out_specs = P(("grp", "dev"), None)
    return jax.shard_map(local, mesh=mesh, in_specs=in_specs, out_specs=out_specs, check_vma=False)
```
